32 devices in a mesh: blk: 8 (over z, y), labels: 4 (over x, core).
Axes of the slice: x: 2, y: 2, z: 4, core: 2. Of those that a mesh axis runs over, the one named last changes fastest.
Arguments:
- features: bfloat16 [6144, 4096], P('blk'), may hold values from -0.099609375 to 0.099609375
- positives: int32 [6144, 8], P('blk'), may hold values from 0 to 16383
- tile_rows: int32 [128, 4], P(('labels', 'blk')), may hold values from 0 to 31, as said below
- tile_count: int32 [128], P(('labels', 'blk')), may hold values from 1 to 4, as said below
- weight: float32 [128, 4, 128, 128], P(('labels', 'blk')), may hold values from -96 to 96
- first_moment: float32 [128, 4, 128, 128], P(('labels', 'blk')), may hold values from -3 to 3
- second_moment: float32 [128, 4, 128, 128], P(('labels', 'blk')), may hold values from 0.05 to 2
Outputs:
- new_weight: float32 [128, 4, 128, 128], P(('labels', 'blk'))
- new_first: float32 [128, 4, 128, 128], P(('labels', 'blk'))
- new_second: float32 [128, 4, 128, 128], P(('labels', 'blk'))
The draws below stay inside these ranges and needn't reach their ends.
Inputs may be any that keep to these rules, and one draw needn't show every extreme that they name: `tile_rows`: in each column block the 4 entries are distinct tile rows; only the first tile_count entries name kept tiles. `tile_count`: every column block keeps at least one tile.
All inputs are finite; a program needn't handle non-finite values.
Results may differ from the reference program's by a relative error of at most 0.0003.
Values may be sent and summed in bfloat16 or wider, within the bound.
A program may use at most 64 MiB of HBM per device.

```python
import math
import jax
import jax.numpy as jnp
import numpy as np
from jax import lax

D = 4096
TILE = 128
KMAX = 4
POS = 8
TILE_ROWS = 32
NCB = 128
LABELS = 16384
ROWS = 6144


def draw_tile_rows(key, part):
    scores = jax.random.randint(key, (NCB, TILE_ROWS), 0, 2 ** 20) * TILE_ROWS
    scores = scores + jnp.arange(TILE_ROWS, dtype=jnp.int32)[None, :]
    order = jnp.argsort(scores, axis=1)
    return order[:, :KMAX].astype(jnp.int32)


def draw_tile_count(key, part):
    counts = jax.random.randint(key, (NCB,), 1, KMAX + 1)
    spot = jax.random.randint(jax.random.fold_in(key, 7), (), 0, NCB)
    return counts.at[spot].set(KMAX).astype(jnp.int32)


def with_ends(result, own_key, smallest, high):
    index_at = [jax.random.randint(jax.random.fold_in(own_key, axis), (), 0, length) for axis, length in enumerate(result.shape)]
    widest = result.shape.index(max(result.shape))
    beside = index_at[:widest] + [(index_at[widest] + 1) % result.shape[widest]] + index_at[widest + 1:]
    return result.at[tuple(index_at)].set(smallest).at[tuple(beside)].set(high)


def levels(rng, shape, split, smallest, high):
    loudness = 1.0
    for dim, shards_of in split:
        draws = jax.random.uniform(jax.random.fold_in(jax.random.fold_in(rng, 6), dim), (shards_of,), jnp.float32, smallest / len(split), high / len(split))
        loudness = loudness * jnp.repeat(jnp.exp(draws), shape[dim] // shards_of).reshape((-1,) + (1,) * (len(shape) - 1 - dim))
    return loudness


def rank_table(number_of, skew):
    loads = [(1 << 20) // math.isqrt(grade ** skew) + 1 for grade in range(1, number_of + 1)]
    scale = 1 + sum(loads) // (1 << 30)
    return np.cumsum(np.array([max(1, weight // scale) for weight in loads]))


def skewed_ids(stream_key, dims, amount, skew):
    table = rank_table(amount, skew)
    pick = jax.random.randint(jax.random.fold_in(stream_key, 1), dims, 0, int(table[amount - 1]))
    grade = jnp.searchsorted(jnp.asarray(table, jnp.int32), pick, side="right")
    return jax.random.permutation(jax.random.fold_in(stream_key, 2), amount)[grade].astype(jnp.int32)


def bell_draw(stream_key, dims, deviation, most, shards=(), kind=jnp.bfloat16):
    result = deviation * jax.random.normal(stream_key, dims, jnp.float32)
    if shards:
        result = result * levels(stream_key, dims, shards, -0.22, 0.18)
    return jnp.clip(result, -most, most).astype(kind)


def setup_inputs(seed: int = 0) -> dict:
    arg_keys = jax.random.split(jax.random.key(seed), 8)
    features = bell_draw(arg_keys[0], (ROWS, D), 0.015625, 0.099609375, ((0, 8),))
    positives = with_ends(skewed_ids(arg_keys[1], (ROWS, POS), LABELS, 2), jax.random.fold_in(arg_keys[1], 3), 0, LABELS - 1).astype(jnp.int32)
    tile_rows = draw_tile_rows(jax.random.fold_in(arg_keys[7], 71), 0)
    tile_count = draw_tile_count(jax.random.fold_in(arg_keys[7], 71), 0)
    weight = bell_draw(arg_keys[4], (NCB, KMAX, TILE, TILE), 16.0, 96.0, ((0, 32),), jnp.float32)
    first_moment = bell_draw(arg_keys[5], (NCB, KMAX, TILE, TILE), 0.5, 3.0, ((0, 32),), jnp.float32)
    second_moment = jnp.clip(jnp.exp(math.log(2.0) - 3.6888794 * jax.random.uniform(arg_keys[6], (NCB, KMAX, TILE, TILE), jnp.float32) ** levels(arg_keys[6], (NCB, KMAX, TILE, TILE), ((0, 32),), -0.2, 0.2)), 0.05, 2.0)
    return {"features": features, "positives": positives, "tile_rows": tile_rows, "tile_count": tile_count, "weight": weight, "first_moment": first_moment, "second_moment": second_moment}


beta_one = 0.9
beta_two = 0.999
adam_eps = 1e-08
learn_rate = 0.1
correction_one = 1.0 - 0.9 ** 10
correction_two = 1.0 - 0.999 ** 10

def reference(features, positives, tile_rows, tile_count, weight, first_moment, second_moment):
    total_rows = features.shape[0]
    tile_split = features.reshape(total_rows, D // TILE, TILE)
    slot_ids = jnp.arange(KMAX, dtype=jnp.int32)

    def one_block(block_args):
        block_index, row_ids, slot_count, block_weight = block_args
        live_mask = (slot_ids < slot_count).astype(jnp.float32)
        chosen = jnp.take(tile_split, row_ids.astype(jnp.int32), axis=1).astype(jnp.float32)
        rounded = lax.optimization_barrier(block_weight.astype(jnp.bfloat16))
        w_masked = rounded.astype(jnp.float32) * live_mask[:, None, None]
        logits = jnp.einsum('rsk,skt->rt', chosen, w_masked)
        label_ids = block_index * TILE + jnp.arange(TILE, dtype=jnp.int32)
        targets = jnp.any(positives[:, :, None] == label_ids[None, None, :], axis=1).astype(jnp.float32)
        residual = lax.optimization_barrier((jax.nn.sigmoid(logits) - targets).astype(jnp.bfloat16))
        return jnp.einsum('rsk,rt->skt', chosen, residual.astype(jnp.float32))
    gradient = lax.map(one_block, (jnp.arange(NCB, dtype=jnp.int32), tile_rows, tile_count, weight))
    kept = (slot_ids[None, :] < tile_count[:, None])[:, :, None, None]
    moved_first = beta_one * first_moment + (1.0 - beta_one) * gradient
    moved_second = beta_two * second_moment + (1.0 - beta_two) * gradient * gradient
    step_dir = moved_first / correction_one / (jnp.sqrt(moved_second / correction_two) + adam_eps)
    moved_weight = weight - learn_rate * step_dir
    new_weight = jnp.where(kept, moved_weight, weight)
    new_first = jnp.where(kept, moved_first, first_moment)
    new_second = jnp.where(kept, moved_second, second_moment)
    return (new_weight, new_first, new_second)
```

```python
import functools

import jax
import jax.numpy as jnp
from jax import lax
from jax.experimental import pallas as pl
from jax.experimental.pallas import tpu as pltpu
from jax.sharding import PartitionSpec as P

beta_one = 0.9
beta_two = 0.999
adam_eps = 1e-08
learn_rate = 0.1
correction_one = 1.0 - 0.9**10
correction_two = 1.0 - 0.999**10

F32 = jnp.float32
BF16 = jnp.bfloat16


def grad_kernel(
    blk, labels, own, slots, side, chunks,
    feat_in, tiles, pos, meta,
    grad,
    feat, feat2, pos2, tiles_in, meta_in, rows_s, acc, acc_in,
    y_send, y_recv, p_sem, x_send, x_recv, t_send, t_recv, m_send, m_recv, s_sem, g_send, g_recv, f_sem,
):
    me = lax.axis_index("blk")
    lab = lax.axis_index("labels")
    ring = blk // 2
    zed, par = me // 2, lax.rem(me, 2)
    partner = zed * 2 + (1 - par)
    cols, row_total, _ = feat.shape
    part = row_total // labels
    sub = part // chunks
    bits = []
    while (1 << len(bits)) < labels:
        bits.append(1 << len(bits))
    bits = bits[::-1]

    def at(k):
        return lax.rem(zed + k, ring) * 2 + par

    def flip(index, bit):
        return index + bit * (1 - 2 * lax.rem(index // bit, 2))

    def flip_all(mask):
        index = lab
        for bit in bits:
            if mask & bit:
                index = flip(index, bit)
        return index

    loads = [
        pltpu.make_async_copy(feat_in.at[:, pl.ds(j * side, side)], feat.at[j], f_sem.at[j])
        for j in range(cols)
    ]
    for load in loads:
        load.start()
    barrier = pltpu.get_barrier_semaphore()
    peers = [{"blk": partner}] + [{"blk": at(k)} for k in range(1, ring)]
    peers += [{"labels": flip(lab, bit)} for bit in bits]
    for peer in peers:
        pl.semaphore_signal(barrier, inc=1, device_id=peer, device_id_type=pl.DeviceIdType.MESH)
    pl.semaphore_wait(barrier, len(peers))

    def remote(src, dst, send, recv, peer):
        return pltpu.make_async_remote_copy(
            src_ref=src, dst_ref=dst, send_sem=send, recv_sem=recv,
            device_id=peer, device_id_type=pl.DeviceIdType.MESH,
        )

    def rows_of(mask, c):
        start = pl.multiple_of(flip_all(mask) * part + c * sub, 16)
        return pl.ds(start, sub)

    m_out, t_out = {}, {}
    for k in range(1, ring):
        m_out[k] = remote(meta, meta_in.at[k], m_send.at[k], m_recv.at[k], {"blk": at(k)})
        m_out[k].start()
    for load in loads:
        load.wait()
    y_out = []
    p_out = remote(pos, pos2, p_sem.at[0], p_sem.at[1], {"blk": partner})
    p_out.start()
    for c in range(chunks):
        rows = rows_of(0, c)
        y_out.append(remote(feat.at[:, rows], feat2.at[:, rows], y_send.at[c], y_recv.at[c], {"blk": partner}))
        y_out[c].start()
    for k in range(1, ring):
        t_out[k] = remote(tiles, tiles_in.at[k], t_send.at[k], t_recv.at[k], {"blk": at(k)})
        t_out[k].start()
    own_rows = pltpu.make_async_copy(meta, rows_s.at[0], s_sem.at[0])
    own_rows.start()
    own_rows.wait()

    x_out = {}

    def masks_before(step):
        found = [0]
        for bit in bits[:step]:
            found = found + [m | bit for m in found]
        return found

    def send_on(step, mask, c):
        slot = (mask | bits[step], c)
        sem = slot[0] * chunks + c
        rows = rows_of(mask, c)
        x_out[slot] = remote(
            feat2.at[:, rows], feat2.at[:, rows], x_send.at[sem], x_recv.at[sem],
            {"labels": flip(lab, bits[step])},
        )
        x_out[slot].start()

    def take_on(mask, c):
        sem = mask * chunks + c
        rows = rows_of(mask, c)
        pltpu.make_async_remote_copy(
            src_ref=feat2.at[:, rows], dst_ref=feat2.at[:, rows], send_sem=x_send.at[sem],
            recv_sem=x_recv.at[sem], device_id={"labels": flip(lab, mask & -mask)},
            device_id_type=pl.DeviceIdType.MESH,
        ).wait_recv()

    def relay(stage, c):
        if stage == 0:
            y_out[c].wait_recv()
            for step in range(len(bits)):
                send_on(step, 0, c)
            return
        low = bits[stage - 1]
        for m in masks_before(stage - 1):
            take_on(m | low, c)
            for step in range(stage, len(bits)):
                send_on(step, m | low, c)

    label_iota = lax.broadcasted_iota(jnp.int32, (side, 1), 0)
    step_rows = 256 if row_total % 256 == 0 else row_total

    def owner_pass(slab, slab_pos, k, tile_ref, first):
        owner = lax.rem(zed - k + ring, ring) * 2 + par
        base = (lab * blk + owner) * own * side

        def block(b, _):
            wt = tile_ref[b]
            ids = base + b * side + label_iota
            at_rows = [rows_s[k, 0, b * slots + s] for s in range(slots)]
            total = None
            for r in range(0, row_total, step_rows):
                chosen = jnp.concatenate(
                    [slab[col, r:r + step_rows, :] for col in at_rows], axis=1
                )
                logits = lax.dot_general(
                    wt, chosen, (((1,), (1,)), ((), ())), preferred_element_type=F32
                )
                hit = None
                for p in range(slab_pos.shape[0]):
                    same = slab_pos[p:p + 1, r:r + step_rows] == ids
                    hit = same if hit is None else hit | same
                resid = (jax.nn.sigmoid(logits) - jnp.where(hit, 1.0, 0.0)).astype(BF16)
                term = jnp.dot(resid, chosen, preferred_element_type=F32)
                total = term if total is None else total + term
            if first:
                acc[k, b] = total
            else:
                acc[k, b] += total
            return 0

        lax.fori_loop(0, own, block, 0)

    stages = len(bits) + 1
    todo = sorted(((c + s, s, c) for c in range(chunks) for s in range(stages)), key=lambda x: (x[0], x[1]))
    todo = [(s, c) for _, s, c in todo]
    share = max(1, len(todo) // (ring + 1))

    owner_pass(feat, pos, 0, tiles, True)
    for k in range(1, ring):
        for _ in range(share):
            relay(*todo.pop(0))
        m_out[k].wait_recv()
        t_out[k].wait_recv()
        row_copy = pltpu.make_async_copy(meta_in.at[k], rows_s.at[k], s_sem.at[k])
        row_copy.start()
        row_copy.wait()
        owner_pass(feat, pos, k, tiles_in.at[k], True)
    while todo:
        relay(*todo.pop(0))
    p_out.wait_recv()

    g_out = {}
    for k in list(range(1, ring)):
        owner_pass(feat2, pos2, k, tiles_in.at[k], False)
        g_out[k] = remote(
            acc.at[k], acc_in.at[k], g_send.at[k], g_recv.at[k],
            {"blk": lax.rem(zed - k + ring, ring) * 2 + par},
        )
        g_out[k].start()
    owner_pass(feat2, pos2, 0, tiles, False)
    for k in range(1, ring):
        g_out[k].wait_recv()

    def finish(b, _):
        total = acc[0, b]
        for k in range(1, ring):
            total = total + acc_in[k, b]
        for s in range(slots):
            grad[b, s] = total[:, s * side:(s + 1) * side].T
        return 0

    lax.fori_loop(0, own, finish, 0)
    for k in range(1, ring):
        m_out[k].wait_send()
        t_out[k].wait_send()
        g_out[k].wait_send()
    p_out.wait_send()
    for c in range(chunks):
        y_out[c].wait_send()
    for copy in x_out.values():
        copy.wait_send()


def local(blk, labels, features, positives, tile_rows, tile_count, weight, first_moment, second_moment):
    own, slots, side, _ = weight.shape
    ring = blk // 2
    row_total = features.shape[0]
    cols = features.shape[1] // side
    slot_ids = jnp.arange(slots, dtype=jnp.int32)
    kept = (slot_ids[None, :] < tile_count[:, None])[:, :, None, None]
    masked = jnp.where(kept, weight, 0.0).astype(BF16)
    tiles = masked.transpose(0, 3, 1, 2).reshape(own, side, slots * side)
    meta = jnp.pad(tile_rows.reshape(1, own * slots), ((0, 7), (0, 128 - own * slots)))
    pos = positives.T
    part = row_total // labels
    chunks = next(c for c in (4, 3, 2, 1) if part % (16 * c) == 0)
    vmem = pl.BlockSpec(memory_space=pltpu.VMEM)
    dma = pltpu.SemaphoreType.DMA
    gradient = pl.pallas_call(
        functools.partial(grad_kernel, blk, labels, own, slots, side, chunks),
        out_shape=jax.ShapeDtypeStruct(weight.shape, F32),
        in_specs=[pl.BlockSpec(memory_space=pl.ANY)] + [vmem] * 3,
        out_specs=vmem,
        scratch_shapes=[
            pltpu.VMEM((cols, row_total, side), BF16),
            pltpu.VMEM((cols, row_total, side), BF16),
            pltpu.VMEM(pos.shape, jnp.int32),
            pltpu.VMEM((ring,) + tiles.shape, BF16),
            pltpu.VMEM((ring,) + meta.shape, jnp.int32),
            pltpu.SMEM((ring,) + meta.shape, jnp.int32),
            pltpu.VMEM((ring,) + tiles.shape, F32),
            pltpu.VMEM((ring,) + tiles.shape, F32),
            dma((chunks,)), dma((chunks,)), dma((2,)),
            dma((labels * chunks,)), dma((labels * chunks,)),
            dma((ring,)), dma((ring,)), dma((ring,)), dma((ring,)), dma((ring,)),
            dma((ring,)), dma((ring,)), dma((cols,)),
        ],
        compiler_params=pltpu.CompilerParams(collective_id=0, has_side_effects=True),
    )(features, tiles, pos, meta)
    moved_first = beta_one * first_moment + (1.0 - beta_one) * gradient
    moved_second = beta_two * second_moment + (1.0 - beta_two) * gradient * gradient
    step_dir = moved_first / correction_one / (jnp.sqrt(moved_second / correction_two) + adam_eps)
    moved_weight = weight - learn_rate * step_dir
    new_weight = jnp.where(kept, moved_weight, weight)
    new_first = jnp.where(kept, moved_first, first_moment)
    new_second = jnp.where(kept, moved_second, second_moment)
    return (new_weight, new_first, new_second)


def solution(mesh):
    owner = P(("labels", "blk"), None, None, None)
    return jax.shard_map(
        functools.partial(local, mesh.shape["blk"], mesh.shape["labels"]),
        mesh=mesh,
        in_specs=(
            P("blk", None),
            P("blk", None),
            P(("labels", "blk"), None),
            P(("labels", "blk")),
            owner, owner, owner,
        ),
        out_specs=(owner, owner, owner),
        check_vma=False,
    )
```

```python
import functools

import jax
import jax.numpy as jnp
from jax import lax
from jax.experimental import pallas as pl
from jax.experimental.pallas import tpu as pltpu
from jax.sharding import PartitionSpec as P

beta_one = 0.9
beta_two = 0.999
adam_eps = 1e-08
learn_rate = 0.1
correction_one = 1.0 - 0.9**10
correction_two = 1.0 - 0.999**10

F32 = jnp.float32
BF16 = jnp.bfloat16


def grad_kernel(
    blk, labels, own, slots, side, chunks,
    feat_in, tiles, pos, meta,
    grad,
    feat, feat2, pos2, tiles_in, meta_in, rows_s, acc, acc_in,
    y_send, y_recv, p_sem, x_send, x_recv, t_send, t_recv, m_send, m_recv, s_sem, g_send, g_recv, f_sem,
):
    me = lax.axis_index("blk")
    lab = lax.axis_index("labels")
    ring = blk // 2
    zed, par = me // 2, lax.rem(me, 2)
    partner = zed * 2 + (1 - par)
    cols, row_total, _ = feat.shape
    part = row_total // labels
    sub = part // chunks
    bits = []
    while (1 << len(bits)) < labels:
        bits.append(1 << len(bits))
    bits = bits[::-1]

    def at(k):
        return lax.rem(zed + k, ring) * 2 + par

    def flip(index, bit):
        return index + bit * (1 - 2 * lax.rem(index // bit, 2))

    def flip_all(mask):
        index = lab
        for bit in bits:
            if mask & bit:
                index = flip(index, bit)
        return index

    loads = [
        pltpu.make_async_copy(feat_in.at[:, pl.ds(j * side, side)], feat.at[j], f_sem.at[j])
        for j in range(cols)
    ]
    for load in loads:
        load.start()
    barrier = pltpu.get_barrier_semaphore()
    peers = [{"blk": partner}] + [{"blk": at(k)} for k in range(1, ring)]
    peers += [{"labels": flip(lab, bit)} for bit in bits]
    for peer in peers:
        pl.semaphore_signal(barrier, inc=1, device_id=peer, device_id_type=pl.DeviceIdType.MESH)
    pl.semaphore_wait(barrier, len(peers))

    def remote(src, dst, send, recv, peer):
        return pltpu.make_async_remote_copy(
            src_ref=src, dst_ref=dst, send_sem=send, recv_sem=recv,
            device_id=peer, device_id_type=pl.DeviceIdType.MESH,
        )

    def rows_of(mask, c):
        start = pl.multiple_of(flip_all(mask) * part + c * sub, 16)
        return pl.ds(start, sub)

    m_out = {}
    for k in range(1, ring):
        m_out[k] = remote(meta, meta_in.at[k], m_send.at[k], m_recv.at[k], {"blk": at(k)})
        m_out[k].start()

    def beside(way):
        return {"blk": (zed + 1 - 2 * way) * 2 + par}

    def tile_copy(way, d):
        owner = zed - d + 2 * d * way
        src = tiles if d == 0 else tiles_in.at[owner]
        return remote(src, tiles_in.at[owner], t_send.at[way, d], t_recv.at[way, d + 1], beside(way))

    def has(way, d):
        return zed >= d if way == 0 else zed + d < ring

    def sends_tile(way, d):
        return has(way, d) & has(1 - way, 1)

    def send_tile(way, d):
        if d + 1 >= ring:
            return

        @pl.when(sends_tile(way, d))
        def _():
            tile_copy(way, d).start()

    def take_tile(way, d):
        @pl.when(has(way, d))
        def _():
            owner = zed - d + 2 * d * way
            remote(
                tiles_in.at[owner], tiles_in.at[owner], t_send.at[way, d], t_recv.at[way, d], beside(way)
            ).wait_recv()

    for way in range(2):
        send_tile(way, 0)
    for load in loads:
        load.wait()
    y_out = []
    p_out = remote(pos, pos2, p_sem.at[0], p_sem.at[1], {"blk": partner})
    p_out.start()
    for c in range(chunks):
        rows = rows_of(0, c)
        y_out.append(remote(feat.at[:, rows], feat2.at[:, rows], y_send.at[c], y_recv.at[c], {"blk": partner}))
        y_out[c].start()
    own_rows = pltpu.make_async_copy(meta, rows_s.at[zed], s_sem.at[0])
    own_rows.start()
    own_rows.wait()

    x_out = {}

    def masks_before(step):
        found = [0]
        for bit in bits[:step]:
            found = found + [m | bit for m in found]
        return found

    def send_on(step, mask, c):
        slot = (mask | bits[step], c)
        sem = slot[0] * chunks + c
        rows = rows_of(mask, c)
        x_out[slot] = remote(
            feat2.at[:, rows], feat2.at[:, rows], x_send.at[sem], x_recv.at[sem],
            {"labels": flip(lab, bits[step])},
        )
        x_out[slot].start()

    def take_on(mask, c):
        sem = mask * chunks + c
        rows = rows_of(mask, c)
        pltpu.make_async_remote_copy(
            src_ref=feat2.at[:, rows], dst_ref=feat2.at[:, rows], send_sem=x_send.at[sem],
            recv_sem=x_recv.at[sem], device_id={"labels": flip(lab, mask & -mask)},
            device_id_type=pl.DeviceIdType.MESH,
        ).wait_recv()

    def relay(stage, c):
        if stage == 0:
            y_out[c].wait_recv()
            for step in range(len(bits)):
                send_on(step, 0, c)
            return
        low = bits[stage - 1]
        for m in masks_before(stage - 1):
            take_on(m | low, c)
            for step in range(stage, len(bits)):
                send_on(step, m | low, c)

    label_iota = lax.broadcasted_iota(jnp.int32, (side, 1), 0)
    step_rows = 256 if row_total % 256 == 0 else row_total

    def one_block(slab, slab_pos, owner, tile_ref, first, b):
        base = (lab * blk + owner * 2 + par) * own * side
        if True:
            wt = tile_ref[b]
            ids = base + b * side + label_iota
            at_rows = [rows_s[owner, 0, b * slots + s] for s in range(slots)]
            total = None
            for r in range(0, row_total, step_rows):
                chosen = jnp.concatenate(
                    [slab[col, r:r + step_rows, :] for col in at_rows], axis=1
                )
                logits = lax.dot_general(
                    wt, chosen, (((1,), (1,)), ((), ())), preferred_element_type=F32
                )
                hit = None
                for p in range(slab_pos.shape[0]):
                    same = slab_pos[p:p + 1, r:r + step_rows] == ids
                    hit = same if hit is None else hit | same
                resid = (jax.nn.sigmoid(logits) - jnp.where(hit, 1.0, 0.0)).astype(BF16)
                term = jnp.dot(resid, chosen, preferred_element_type=F32)
                total = term if total is None else total + term
            if first:
                acc[owner, b] = total
            else:
                acc[owner, b] += total

    def owner_pass(slab, slab_pos, owner, tile_ref, first):
        def block(b, _):
            one_block(slab, slab_pos, owner, tile_ref, first, b)
            return 0

        lax.fori_loop(0, own, block, 0)

    stages = len(bits) + 1
    todo = sorted(((c + s, s, c) for c in range(chunks) for s in range(stages)), key=lambda x: (x[0], x[1]))
    def relay_next():
        now = todo[0][0] if todo else None
        while todo and todo[0][0] == now:
            _, stage, c = todo.pop(0)
            relay(stage, c)

    owner_pass(feat, pos, zed, tiles, True)
    for k in range(1, ring):
        m_out[k].wait_recv()
        row_copy = pltpu.make_async_copy(
            meta_in.at[k], rows_s.at[lax.rem(zed - k + ring, ring)], s_sem.at[k]
        )
        row_copy.start()
        row_copy.wait()
    relay_next()
    for d in range(1, ring):
        for way in range(2):
            take_tile(way, d)
            send_tile(way, d)
        for way in range(2):
            @pl.when(has(way, d))
            def _():
                owner = zed - d + 2 * d * way
                owner_pass(feat, pos, owner, tiles_in.at[owner], True)

            relay_next()
    while todo:
        relay_next()
    p_out.wait_recv()

    def sum_copy(way, owner, b):
        return remote(
            acc.at[owner, b], acc_in.at[way, owner, b],
            g_send.at[way, owner, b], g_recv.at[way, owner, b], beside(way),
        )

    def passes(way, step):
        owner = ring - 1 - step if way == 0 else step
        return owner, (zed < owner if way == 0 else zed > owner)

    for step in range(ring - 1):
        def hop(b, _):
            for way in range(2):
                owner, goes = passes(way, step)

                @pl.when(goes)
                def _():
                    one_block(feat2, pos2, owner, tiles_in.at[owner], False, b)

                    @pl.when(has(way, 1))
                    def _():
                        sum_copy(way, owner, b).wait_recv()
                        acc[owner, b] += acc_in[way, owner, b]

                    sum_copy(way, owner, b).start()
            return 0

        lax.fori_loop(0, own, hop, 0)
    owner_pass(feat2, pos2, zed, tiles, False)

    def finish(b, _):
        for way in range(2):
            @pl.when(has(way, 1))
            def _():
                sum_copy(way, zed, b).wait_recv()
                acc[zed, b] += acc_in[way, zed, b]

        total = acc[zed, b]
        for s in range(slots):
            grad[b, s] = total[:, s * side:(s + 1) * side].T
        return 0

    lax.fori_loop(0, own, finish, 0)
    for k in range(1, ring):
        m_out[k].wait_send()
    for way in range(2):
        for d in range(ring - 1):
            @pl.when(sends_tile(way, d))
            def _():
                tile_copy(way, d).wait_send()
        for step in range(ring - 1):
            owner, goes = passes(way, step)

            @pl.when(goes)
            def _():
                def sent(b, _):
                    sum_copy(way, owner, b).wait_send()
                    return 0

                lax.fori_loop(0, own, sent, 0)
    p_out.wait_send()
    for c in range(chunks):
        y_out[c].wait_send()
    for copy in x_out.values():
        copy.wait_send()


def local(blk, labels, features, positives, tile_rows, tile_count, weight, first_moment, second_moment):
    own, slots, side, _ = weight.shape
    ring = blk // 2
    row_total = features.shape[0]
    cols = features.shape[1] // side
    slot_ids = jnp.arange(slots, dtype=jnp.int32)
    kept = (slot_ids[None, :] < tile_count[:, None])[:, :, None, None]
    masked = jnp.where(kept, weight, 0.0).astype(BF16)
    tiles = masked.transpose(0, 3, 1, 2).reshape(own, side, slots * side)
    meta = jnp.pad(tile_rows.reshape(1, own * slots), ((0, 7), (0, 128 - own * slots)))
    pos = positives.T
    part = row_total // labels
    chunks = next(c for c in (6, 4, 3, 2, 1) if part % (16 * c) == 0)
    vmem = pl.BlockSpec(memory_space=pltpu.VMEM)
    dma = pltpu.SemaphoreType.DMA
    gradient = pl.pallas_call(
        functools.partial(grad_kernel, blk, labels, own, slots, side, chunks),
        out_shape=jax.ShapeDtypeStruct(weight.shape, F32),
        in_specs=[pl.BlockSpec(memory_space=pl.ANY)] + [vmem] * 3,
        out_specs=vmem,
        scratch_shapes=[
            pltpu.VMEM((cols, row_total, side), BF16),
            pltpu.VMEM((cols, row_total, side), BF16),
            pltpu.VMEM(pos.shape, jnp.int32),
            pltpu.VMEM((ring,) + tiles.shape, BF16),
            pltpu.VMEM((ring,) + meta.shape, jnp.int32),
            pltpu.SMEM((ring,) + meta.shape, jnp.int32),
            pltpu.VMEM((ring,) + tiles.shape, F32),
            pltpu.VMEM((2, ring) + tiles.shape, F32),
            dma((chunks,)), dma((chunks,)), dma((2,)),
            dma((labels * chunks,)), dma((labels * chunks,)),
            dma((2, ring)), dma((2, ring)), dma((ring,)), dma((ring,)), dma((ring,)),
            dma((2, ring, own)), dma((2, ring, own)), dma((cols,)),
        ],
        compiler_params=pltpu.CompilerParams(collective_id=0, has_side_effects=True),
    )(features, tiles, pos, meta)
    moved_first = beta_one * first_moment + (1.0 - beta_one) * gradient
    moved_second = beta_two * second_moment + (1.0 - beta_two) * gradient * gradient
    step_dir = moved_first / correction_one / (jnp.sqrt(moved_second / correction_two) + adam_eps)
    moved_weight = weight - learn_rate * step_dir
    new_weight = jnp.where(kept, moved_weight, weight)
    new_first = jnp.where(kept, moved_first, first_moment)
    new_second = jnp.where(kept, moved_second, second_moment)
    return (new_weight, new_first, new_second)


def solution(mesh):
    owner = P(("labels", "blk"), None, None, None)
    return jax.shard_map(
        functools.partial(local, mesh.shape["blk"], mesh.shape["labels"]),
        mesh=mesh,
        in_specs=(
            P("blk", None),
            P("blk", None),
            P(("labels", "blk"), None),
            P(("labels", "blk")),
            owner, owner, owner,
        ),
        out_specs=(owner, owner, owner),
        check_vma=False,
    )
```

```python
import functools

import jax
import jax.numpy as jnp
from jax import lax
from jax.experimental import pallas as pl
from jax.experimental.pallas import tpu as pltpu
from jax.sharding import PartitionSpec as P

beta_one = 0.9
beta_two = 0.999
adam_eps = 1e-08
learn_rate = 0.1
correction_one = 1.0 - 0.9**10
correction_two = 1.0 - 0.999**10

F32 = jnp.float32
BF16 = jnp.bfloat16


def grad_kernel(
    blk, labels, own, slots, side, chunks,
    feat_in, tiles, pos, meta,
    grad,
    feat, feat2, pos2, tiles_in, meta_in, rows_s, acc, acc_in,
    y_send, y_recv, p_sem, x_send, x_recv, t_send, t_recv, m_send, m_recv, s_sem, g_send, g_recv, f_sem,
):
    me = lax.axis_index("blk")
    lab = lax.axis_index("labels")
    ring = blk // 2
    zed, par = me // 2, lax.rem(me, 2)
    partner = zed * 2 + (1 - par)
    cols, row_total, _ = feat.shape
    part = row_total // labels
    sub = part // chunks
    bits = []
    while (1 << len(bits)) < labels:
        bits.append(1 << len(bits))
    bits = bits[::-1]

    def at(k):
        return lax.rem(zed + k, ring) * 2 + par

    def flip(index, bit):
        return index + bit * (1 - 2 * lax.rem(index // bit, 2))

    def flip_all(mask):
        index = lab
        for bit in bits:
            if mask & bit:
                index = flip(index, bit)
        return index

    loads = [
        pltpu.make_async_copy(feat_in.at[:, pl.ds(j * side, side)], feat.at[j], f_sem.at[j])
        for j in range(cols)
    ]
    for load in loads:
        load.start()
    barrier = pltpu.get_barrier_semaphore()
    peers = [{"blk": partner}] + [{"blk": at(k)} for k in range(1, ring)]
    peers += [{"labels": flip(lab, bit)} for bit in bits]
    for peer in peers:
        pl.semaphore_signal(barrier, inc=1, device_id=peer, device_id_type=pl.DeviceIdType.MESH)
    pl.semaphore_wait(barrier, len(peers))

    def remote(src, dst, send, recv, peer):
        return pltpu.make_async_remote_copy(
            src_ref=src, dst_ref=dst, send_sem=send, recv_sem=recv,
            device_id=peer, device_id_type=pl.DeviceIdType.MESH,
        )

    def rows_of(mask, c):
        start = pl.multiple_of(flip_all(mask) * part + c * sub, 16)
        return pl.ds(start, sub)

    m_out = {}
    for k in range(1, ring):
        m_out[k] = remote(meta, meta_in.at[k], m_send.at[k], m_recv.at[k], {"blk": at(k)})
        m_out[k].start()

    def beside(way):
        return {"blk": (zed + 1 - 2 * way) * 2 + par}

    def tile_copy(way, d):
        owner = zed - d + 2 * d * way
        src = tiles if d == 0 else tiles_in.at[owner]
        return remote(src, tiles_in.at[owner], t_send.at[way, d], t_recv.at[way, d + 1], beside(way))

    def has(way, d):
        return zed >= d if way == 0 else zed + d < ring

    def sends_tile(way, d):
        return has(way, d) & has(1 - way, 1)

    def send_tile(way, d):
        if d + 1 >= ring:
            return

        @pl.when(sends_tile(way, d))
        def _():
            tile_copy(way, d).start()

    def take_tile(way, d):
        @pl.when(has(way, d))
        def _():
            owner = zed - d + 2 * d * way
            remote(
                tiles_in.at[owner], tiles_in.at[owner], t_send.at[way, d], t_recv.at[way, d], beside(way)
            ).wait_recv()

    for way in range(2):
        send_tile(way, 0)
    for load in loads:
        load.wait()
    y_out = []
    p_out = remote(pos, pos2, p_sem.at[0], p_sem.at[1], {"blk": partner})
    p_out.start()
    for c in range(chunks):
        rows = rows_of(0, c)
        y_out.append(remote(feat.at[:, rows], feat2.at[:, rows], y_send.at[c], y_recv.at[c], {"blk": partner}))
        y_out[c].start()
    own_rows = pltpu.make_async_copy(meta, rows_s.at[zed], s_sem.at[0])
    own_rows.start()
    own_rows.wait()

    x_out = {}

    def masks_before(step):
        found = [0]
        for bit in bits[:step]:
            found = found + [m | bit for m in found]
        return found

    def send_on(step, mask, c):
        slot = (mask | bits[step], c)
        sem = slot[0] * chunks + c
        rows = rows_of(mask, c)
        x_out[slot] = remote(
            feat2.at[:, rows], feat2.at[:, rows], x_send.at[sem], x_recv.at[sem],
            {"labels": flip(lab, bits[step])},
        )
        x_out[slot].start()

    def take_on(mask, c):
        sem = mask * chunks + c
        rows = rows_of(mask, c)
        pltpu.make_async_remote_copy(
            src_ref=feat2.at[:, rows], dst_ref=feat2.at[:, rows], send_sem=x_send.at[sem],
            recv_sem=x_recv.at[sem], device_id={"labels": flip(lab, mask & -mask)},
            device_id_type=pl.DeviceIdType.MESH,
        ).wait_recv()

    def relay(stage, c):
        if stage == 0:
            y_out[c].wait_recv()
            for step in range(len(bits)):
                send_on(step, 0, c)
            return
        low = bits[stage - 1]
        for m in masks_before(stage - 1):
            take_on(m | low, c)
            for step in range(stage, len(bits)):
                send_on(step, m | low, c)

    label_iota = lax.broadcasted_iota(jnp.int32, (side, 1), 0)
    step_rows = 256 if row_total % 256 == 0 else row_total

    def one_block(slab, slab_pos, owner, tile_ref, first, b):
        base = (lab * blk + owner * 2 + par) * own * side
        if True:
            wt = tile_ref[b]
            ids = base + b * side + label_iota
            at_rows = [rows_s[owner, 0, b * slots + s] for s in range(slots)]
            total = None
            for r in range(0, row_total, step_rows):
                chosen = jnp.concatenate(
                    [slab[col, r:r + step_rows, :] for col in at_rows], axis=1
                )
                logits = lax.dot_general(
                    wt, chosen, (((1,), (1,)), ((), ())), preferred_element_type=F32
                )
                hit = None
                for p in range(slab_pos.shape[0]):
                    same = slab_pos[p:p + 1, r:r + step_rows] == ids
                    hit = same if hit is None else hit | same
                resid = (jax.nn.sigmoid(logits) - jnp.where(hit, 1.0, 0.0)).astype(BF16)
                term = jnp.dot(resid, chosen, preferred_element_type=F32)
                total = term if total is None else total + term
            if first:
                acc[owner, b] = total
            else:
                acc[owner, b] += total

    def owner_pass(slab, slab_pos, owner, tile_ref, first):
        def block(b, _):
            one_block(slab, slab_pos, owner, tile_ref, first, b)
            return 0

        lax.fori_loop(0, own, block, 0)

    stages = len(bits) + 1
    todo = sorted(((c + s, s, c) for c in range(chunks) for s in range(stages)), key=lambda x: (x[0], x[1]))
    def relay_next():
        now = todo[0][0] if todo else None
        while todo and todo[0][0] == now:
            _, stage, c = todo.pop(0)
            relay(stage, c)

    owner_pass(feat, pos, zed, tiles, True)
    for k in range(1, ring):
        m_out[k].wait_recv()
        row_copy = pltpu.make_async_copy(
            meta_in.at[k], rows_s.at[lax.rem(zed - k + ring, ring)], s_sem.at[k]
        )
        row_copy.start()
        row_copy.wait()
    relay_next()
    for d in range(1, ring):
        for way in range(2):
            take_tile(way, d)
            send_tile(way, d)
        for way in range(2):
            @pl.when(has(way, d))
            def _():
                owner = zed - d + 2 * d * way
                owner_pass(feat, pos, owner, tiles_in.at[owner], True)

            relay_next()
    while todo:
        relay_next()
    p_out.wait_recv()

    def sum_copy(way, owner, b):
        return remote(
            acc.at[owner, b], acc_in.at[way, owner, b],
            g_send.at[way, owner, b], g_recv.at[way, owner, b], beside(way),
        )

    def passes(way, step):
        owner = ring - 1 - step if way == 0 else step
        return owner, (zed < owner if way == 0 else zed > owner)

    for step in range(ring - 1):
        def hop(b, _):
            for way in range(2):
                owner, goes = passes(way, step)

                @pl.when(goes)
                def _():
                    one_block(feat2, pos2, owner, tiles_in.at[owner], False, b)

                    @pl.when(has(way, 1))
                    def _():
                        sum_copy(way, owner, b).wait_recv()
                        acc[owner, b] += acc_in[way, owner, b]

                    sum_copy(way, owner, b).start()
            return 0

        lax.fori_loop(0, own, hop, 0)
    owner_pass(feat2, pos2, zed, tiles, False)

    def finish(b, _):
        for way in range(2):
            @pl.when(has(way, 1))
            def _():
                sum_copy(way, zed, b).wait_recv()
                acc[zed, b] += acc_in[way, zed, b]

        total = acc[zed, b]
        for s in range(slots):
            grad[b, s] = total[:, s * side:(s + 1) * side].T
        return 0

    lax.fori_loop(0, own, finish, 0)
    for k in range(1, ring):
        m_out[k].wait_send()
    for way in range(2):
        for d in range(ring - 1):
            @pl.when(sends_tile(way, d))
            def _():
                tile_copy(way, d).wait_send()
        for step in range(ring - 1):
            owner, goes = passes(way, step)

            @pl.when(goes)
            def _():
                def sent(b, _):
                    sum_copy(way, owner, b).wait_send()
                    return 0

                lax.fori_loop(0, own, sent, 0)
    p_out.wait_send()
    for c in range(chunks):
        y_out[c].wait_send()
    for copy in x_out.values():
        copy.wait_send()


def local(blk, labels, features, positives, tile_rows, tile_count, weight, first_moment, second_moment):
    own, slots, side, _ = weight.shape
    ring = blk // 2
    row_total = features.shape[0]
    cols = features.shape[1] // side
    slot_ids = jnp.arange(slots, dtype=jnp.int32)
    kept = (slot_ids[None, :] < tile_count[:, None])[:, :, None, None]
    masked = jnp.where(kept, weight, 0.0).astype(BF16)
    tiles = masked.transpose(0, 3, 1, 2).reshape(own, side, slots * side)
    meta = jnp.pad(tile_rows.reshape(1, own * slots), ((0, 7), (0, 128 - own * slots)))
    pos = positives.T
    part = row_total // labels
    chunks = next(c for c in (12, 6, 4, 3, 2, 1) if part % (16 * c) == 0)
    vmem = pl.BlockSpec(memory_space=pltpu.VMEM)
    dma = pltpu.SemaphoreType.DMA
    gradient = pl.pallas_call(
        functools.partial(grad_kernel, blk, labels, own, slots, side, chunks),
        out_shape=jax.ShapeDtypeStruct(weight.shape, F32),
        in_specs=[pl.BlockSpec(memory_space=pl.ANY)] + [vmem] * 3,
        out_specs=vmem,
        scratch_shapes=[
            pltpu.VMEM((cols, row_total, side), BF16),
            pltpu.VMEM((cols, row_total, side), BF16),
            pltpu.VMEM(pos.shape, jnp.int32),
            pltpu.VMEM((ring,) + tiles.shape, BF16),
            pltpu.VMEM((ring,) + meta.shape, jnp.int32),
            pltpu.SMEM((ring,) + meta.shape, jnp.int32),
            pltpu.VMEM((ring,) + tiles.shape, F32),
            pltpu.VMEM((2, ring) + tiles.shape, F32),
            dma((chunks,)), dma((chunks,)), dma((2,)),
            dma((labels * chunks,)), dma((labels * chunks,)),
            dma((2, ring)), dma((2, ring)), dma((ring,)), dma((ring,)), dma((ring,)),
            dma((2, ring, own)), dma((2, ring, own)), dma((cols,)),
        ],
        compiler_params=pltpu.CompilerParams(collective_id=0, has_side_effects=True),
    )(features, tiles, pos, meta)
    moved_first = beta_one * first_moment + (1.0 - beta_one) * gradient
    moved_second = beta_two * second_moment + (1.0 - beta_two) * gradient * gradient
    step_dir = moved_first / correction_one / (jnp.sqrt(moved_second / correction_two) + adam_eps)
    moved_weight = weight - learn_rate * step_dir
    new_weight = jnp.where(kept, moved_weight, weight)
    new_first = jnp.where(kept, moved_first, first_moment)
    new_second = jnp.where(kept, moved_second, second_moment)
    return (new_weight, new_first, new_second)


def solution(mesh):
    owner = P(("labels", "blk"), None, None, None)
    return jax.shard_map(
        functools.partial(local, mesh.shape["blk"], mesh.shape["labels"]),
        mesh=mesh,
        in_specs=(
            P("blk", None),
            P("blk", None),
            P(("labels", "blk"), None),
            P(("labels", "blk")),
            owner, owner, owner,
        ),
        out_specs=(owner, owner, owner),
        check_vma=False,
    )
```
